32 devices in a mesh: wave: 8 (over y, x, core), lev: 4 (over z).
Axes of the slice: x: 2, y: 2, z: 4, core: 2. Of those that a mesh axis runs over, the one named last changes fastest.
Arguments:
- spec: bfloat16 [16, 128, 640], P('wave', 'lev'), may hold values from -1.5 to 1.5
- legendre: bfloat16 [16, 1280, 640], P('wave'), may hold values from -0.25 to 0.25
- layer_depth_share: float32 [16], P('lev'), may hold values from 0.5 to 2
- quad_weight: float32 [1280], replicated, may hold values from 8 to 32
- wave_of_slot: int32 [16], P('wave'), may hold values from 0 to 639, as said below
Outputs:
- tendency: bfloat16 [16, 128, 640], P('wave', 'lev')
The draws below stay inside these ranges and needn't reach their ends.
Inputs may be any that keep to these rules, and one draw needn't show every extreme that they name: `wave_of_slot`: slots 2 i and 2 i + 1 hold wavenumbers m and 639 - m; no wavenumber appears twice.
All inputs are finite; a program needn't handle non-finite values.
Results may differ from the reference program's by a relative error of at most 0.0047.
The reference program's roundings to bfloat16 on the way count: a program that leaves them out, or rounds other values in their place, can miss the bound.
Values may be sent and summed in bfloat16 or wider, within the bound.
A program may use at most 128 MiB of HBM per device.

```python
import math
import jax
import jax.numpy as jnp
from jax import lax

LAT = 1280
ORDER_SPAN = 640
QUANTITY_TOTAL = 4
EASTWARD_MODES = 16
LEVELS = 16
COLS = 128
MAXLON = 2576
N_LEV = 4


def draw_wave_of_slot(key, part):
    chosen = jax.random.permutation(key, ORDER_SPAN // 2)[:EASTWARD_MODES // 2].astype(jnp.int32)
    return jnp.stack([chosen, ORDER_SPAN - 1 - chosen], axis=1).reshape(EASTWARD_MODES)


def level_of(own_key, shape, cuts, smallest, high):
    gain, own = 1.0, jax.random.fold_in(own_key, 6)
    for dim, parts in cuts:
        draws = jnp.exp(jax.random.uniform(jax.random.fold_in(own, dim), (parts,), jnp.float32, smallest / len(cuts), high / len(cuts)))
        gain = gain * jnp.repeat(draws, shape[dim] // parts).reshape([-1 if axis == dim else 1 for axis in range(len(shape))])
    return gain


def noise(key, shape, scale, reach, pieces=(), kind=jnp.bfloat16):
    level = level_of(key, shape, pieces, -0.22, 0.18) if pieces else 1.0
    values = jax.random.normal(key, shape, jnp.float32) * scale * level
    return jnp.minimum(jnp.maximum(values, -reach), reach).astype(kind)


def setup_inputs(seed: int = 0) -> dict:
    key_of = jax.random.split(jax.random.key(seed), 6)
    spec = noise(key_of[0], (EASTWARD_MODES, COLS, ORDER_SPAN), EASTWARD_MODES ** -0.5, 1.5, ((0, 8), (1, 4)))
    legendre = noise(key_of[1], (EASTWARD_MODES, LAT, ORDER_SPAN), ORDER_SPAN ** -0.5, 0.25, ((0, 8),))
    layer_depth_share = jnp.clip(jnp.exp(math.log(2.0) - 1.3862944 * jax.random.uniform(key_of[2], (LEVELS,), jnp.float32) ** level_of(key_of[2], (LEVELS,), ((0, 4),), -0.2, 0.2)), 0.5, 2.0)
    quad_weight = jnp.clip(jnp.exp(jax.random.uniform(key_of[3], (LAT,), jnp.float32, math.log(8.0), math.log(32.0))), 8.0, 32.0)
    wave_of_slot = draw_wave_of_slot(jax.random.fold_in(key_of[5], 71), 0)
    return {"spec": spec, "legendre": legendre, "layer_depth_share": layer_depth_share, "quad_weight": quad_weight, "wave_of_slot": wave_of_slot}


full_turn = 2.0 * math.pi


def rate_bundle(eastward_velocity, northward_velocity, local_curl_spin, thermal_state, planetary_rotation_effect, processor_dimension):
    absolute = local_curl_spin + planetary_rotation_effect
    return jnp.stack([absolute * eastward_velocity, absolute * northward_velocity,
                      0.5 * (eastward_velocity * eastward_velocity + northward_velocity * northward_velocity),
                      eastward_velocity * thermal_state], axis=processor_dimension)


def reference(spec, legendre, layer_depth_share, quad_weight, wave_of_slot):
    layers_on_processor = LEVELS // N_LEV
    degree_index = jnp.arange(ORDER_SPAN, dtype=jnp.int32)
    valid_cols = degree_index[None, :] < (ORDER_SPAN - wave_of_slot)[:, None]
    screened_entries = jnp.where(valid_cols[:, None, :], spec, jnp.zeros_like(spec))

    def inverse_one(inputs):
        leg_table, coeffs = inputs
        return jnp.dot(leg_table, coeffs.T, preferred_element_type=jnp.float32).astype(jnp.bfloat16)

    fourier = jnp.moveaxis(lax.map(inverse_one, (legendre, screened_entries)), 1, 0)
    points = jnp.arange(MAXLON, dtype=jnp.int32)
    weight_two = jnp.where(wave_of_slot == 0, 1.0, 2.0).astype(jnp.float32)

    def grid_one(inputs):
        latitude, coeffs = inputs
        length = 20 + 4 * jnp.minimum(latitude, LAT - 1 - latitude)
        length_f = length.astype(jnp.float32)
        phase_int = (wave_of_slot[:, None] * points[None, :]) % length
        angles = phase_int.astype(jnp.float32) * full_turn / length_f
        cosine = jnp.cos(angles)
        sine_vals = jnp.sin(angles)
        resolved = 2 * wave_of_slot < length
        amplitude = jnp.where(resolved, weight_two, 0.0)[:, None]
        split_parts = coeffs.reshape(EASTWARD_MODES, N_LEV, 2, QUANTITY_TOTAL, layers_on_processor)
        real_part = split_parts[:, :, 0].reshape(EASTWARD_MODES, -1)
        imag_part = split_parts[:, :, 1].reshape(EASTWARD_MODES, -1)
        grid_vals = jnp.dot(real_part.T, (amplitude * cosine).astype(jnp.bfloat16), preferred_element_type=jnp.float32)
        grid_vals = grid_vals - jnp.dot(imag_part.T, (amplitude * sine_vals).astype(jnp.bfloat16), preferred_element_type=jnp.float32)
        grid_vals = grid_vals.reshape(N_LEV, QUANTITY_TOTAL, layers_on_processor, MAXLON)
        planetary_rotation_effect = 2.0 * jnp.cos((latitude.astype(jnp.float32) + 0.5) * (math.pi / LAT))
        products = rate_bundle(grid_vals[:, 0], grid_vals[:, 1], grid_vals[:, 2], grid_vals[:, 3], planetary_rotation_effect, 1)
        products = products.astype(jnp.bfloat16).reshape(N_LEV * QUANTITY_TOTAL * layers_on_processor, MAXLON)
        live_mask = (points[None, :] < length) & resolved[:, None]
        cos_back = jnp.where(live_mask, cosine, 0.0).astype(jnp.bfloat16)
        sin_back = jnp.where(live_mask, sine_vals, 0.0).astype(jnp.bfloat16)
        row_scale = quad_weight[latitude] / length_f
        real_back = jnp.dot(products, cos_back.T, preferred_element_type=jnp.float32) * row_scale
        imag_back = -jnp.dot(products, sin_back.T, preferred_element_type=jnp.float32) * row_scale
        merged = jnp.stack([real_back.T.reshape(EASTWARD_MODES, N_LEV, QUANTITY_TOTAL, layers_on_processor),
                            imag_back.T.reshape(EASTWARD_MODES, N_LEV, QUANTITY_TOTAL, layers_on_processor)], axis=2)
        return merged.reshape(EASTWARD_MODES, COLS).astype(jnp.bfloat16)

    tend_rows = lax.map(grid_one, (jnp.arange(LAT, dtype=jnp.int32), fourier))

    def direct_one(inputs):
        leg_table, coeffs = inputs
        return jnp.dot(coeffs.T, leg_table, preferred_element_type=jnp.float32)

    tendency = lax.map(direct_one, (legendre, jnp.moveaxis(tend_rows, 1, 0)))
    thermal_state = screened_entries.reshape(EASTWARD_MODES, N_LEV, 2, QUANTITY_TOTAL, layers_on_processor, ORDER_SPAN)[:, :, :, 3].astype(jnp.float32)
    scaled_entries = thermal_state * layer_depth_share.reshape(N_LEV, 1, layers_on_processor, 1)
    scaled_entries = jnp.moveaxis(scaled_entries, 2, 1).reshape(EASTWARD_MODES, 2, LEVELS, ORDER_SPAN)
    below_sum = jnp.flip(jnp.cumsum(jnp.flip(scaled_entries, 2), 2), 2)
    geopot = jnp.moveaxis(below_sum.reshape(EASTWARD_MODES, 2, N_LEV, layers_on_processor, ORDER_SPAN), 1, 2)
    tendency = tendency.reshape(EASTWARD_MODES, N_LEV, 2, QUANTITY_TOTAL, layers_on_processor, ORDER_SPAN)
    tendency = tendency.at[:, :, :, 2].add(geopot)
    tendency = jnp.where(valid_cols[:, None, None, None, None, :], tendency, 0.0)
    return tendency.reshape(EASTWARD_MODES, COLS, ORDER_SPAN).astype(jnp.bfloat16)
```

```python
import functools
import math

import jax
import jax.numpy as jnp
import numpy as np
from jax import lax
from jax.experimental import pallas as pl
from jax.experimental.pallas import tpu as pltpu
from jax.sharding import PartitionSpec as P

TILES = 4
LANES = 128
NT = (((1,), (1,)), ((), ()))


def taylor(first, count):
    return [(-1.0) ** k / math.factorial(2 * k + first) for k in range(count)]


def horner(square, terms):
    total = jnp.full_like(square, terms[-1])
    for term in reversed(terms[:-1]):
        total = total * square + term
    return total


def turn_trig(steps, length, inverse):
    whole = jnp.floor(steps * inverse + 0.5)
    angle = (steps - whole * length) * inverse * (2.0 * math.pi)
    square = angle * angle
    return horner(square, taylor(0, 10)), angle * horner(square, taylor(1, 10))


def lane_maps(slots, fields, layers):
    order = np.arange(slots * 2 * 2 * fields * layers)
    natural = order.reshape(slots, 2, 2, fields, layers)
    return natural.transpose(0, 2, 3, 1, 4).reshape(-1)


def fourier_stage(dims, spec_ref, leg_ref, live_ref, perm_ref, rows_ref):
    slots, columns, half = dims["slots"], dims["columns"], dims["half"]
    total = jnp.zeros((half, LANES), jnp.float32)
    for slot in range(slots):
        masked = spec_ref[slot] * live_ref[slot]
        for hemi in range(2):
            at = (slot * 2 + hemi) * columns
            pieces = []
            if at:
                pieces.append(jnp.zeros((at, masked.shape[1]), masked.dtype))
            pieces.append(masked)
            if at + columns < LANES:
                pieces.append(jnp.zeros((LANES - at - columns, masked.shape[1]), masked.dtype))
            total += lax.dot_general(
                leg_ref[slot, hemi * half : (hemi + 1) * half, :],
                jnp.concatenate(pieces, 0),
                NT,
                preferred_element_type=jnp.float32,
            )
    rows_ref[...] = jnp.dot(
        total.astype(jnp.bfloat16), perm_ref[...], preferred_element_type=jnp.float32
    )


def split_rows(dims, rows_ref, send_ref):
    quarter, half = dims["quarter"], dims["half"]
    for place in range(dims["groups"]):
        low = rows_ref[place * quarter : (place + 1) * quarter, :]
        top = half - place * quarter
        high = rows_ref[top - quarter : top, :]
        send_ref[place] = jnp.concatenate([low, high], 0).astype(jnp.bfloat16)


def grid_stage(dims, device, waves, quad_ref, cor_ref, get_ref, put_refs, scratch):
    slots, groups, half = dims["slots"], dims["groups"], dims["half"]
    fields, layers, quarter = dims["fields"], dims["layers"], dims["quarter"]
    block, total_lat = dims["block"], 2 * half
    count = 2 * quarter
    width = fields * 2 * layers
    depth = 2 * slots * groups
    state, step, tab, left, mixed, acc = scratch
    chunk = TILES * LANES
    lane = lax.broadcasted_iota(jnp.int32, (groups, LANES), 1)
    south_lane = lane // layers % 2 == 1
    tile_lane = lax.broadcasted_iota(jnp.int32, (slots * groups, LANES), 1)
    tile_lane_f = tile_lane.astype(jnp.float32)
    hemi_row = lax.broadcasted_iota(jnp.int32, (2 * layers, 1), 0) < layers
    size = block * width
    padded = left.shape[0]
    eye = (
        lax.broadcasted_iota(jnp.int32, (padded, padded), 0)
        == lax.broadcasted_iota(jnp.int32, (padded, padded), 1)
    ).astype(jnp.bfloat16)
    mixed[...] = jnp.zeros_like(mixed)
    all_waves = jnp.concatenate(waves, 0)

    def group(number, carry):
        first = number * block
        local = [first + u for u in range(block)]
        dist = [
            jnp.where(r < quarter, device * quarter + r, half - device * quarter - count + r)
            for r in local
        ]
        lengths = [20 + 4 * q for q in dist]
        floats = [length.astype(jnp.float32) for length in lengths]
        for u in range(block):
            inverse = 1.0 / jnp.full((slots * groups, LANES), floats[u], jnp.float32)
            rows = pl.ds(u * slots * groups, slots * groups)
            base = turn_trig(all_waves * tile_lane_f, floats[u], inverse)
            hop = turn_trig(all_waves * float(LANES), floats[u], inverse)
            for part in range(2):
                state[part, rows, :] = base[part]
                step[part, rows, :] = hop[part]
            north = get_ref[pl.ds(local[u], groups, stride=count), :]
            south = get_ref[pl.ds(count - 1 - local[u], groups, stride=count), :]
            both = jnp.where(south_lane, south, north)
            at = u * width
            column = at // LANES * LANES
            offset = at % LANES
            for part in range(2):
                for slot in range(slots):
                    home = (slot * 2 + part) * width
                    wave = waves[slot]
                    weight = jnp.where(wave == 0.0, 1.0, 2.0)
                    weight = jnp.where(2.0 * wave < floats[u], weight, 0.0)
                    if part:
                        weight = -weight
                    shift = (offset - home) % LANES
                    moved = pltpu.roll(both, shift, 1) if shift else both
                    keep = (lane >= offset) & (lane < offset + width)
                    row = u * depth + (part * slots + slot) * groups
                    mixed[row : row + groups, column : column + LANES] = jnp.where(
                        keep, moved * weight, 0.0
                    )
        left[...] = lax.dot_general(
            eye, mixed[...].astype(jnp.bfloat16), NT, preferred_element_type=jnp.float32
        ).astype(jnp.bfloat16)
        acc[...] = jnp.zeros_like(acc)
        cor = [
            jnp.where(hemi_row, cor_ref[dist[u]], cor_ref[total_lat - 1 - dist[u]])
            for u in range(block)
        ]

        def walk(index, carry):
            cosine, sine = state[0], state[1]
            turn_cos, turn_sin = step[0], step[1]
            for t in range(TILES):
                start = index * chunk + t * LANES
                point = tile_lane + start
                for u in range(block):
                    rows = slice(u * slots * groups, (u + 1) * slots * groups)
                    live = point < lengths[u]
                    cols = slice(t * LANES, (t + 1) * LANES)
                    low = u * depth
                    mid = low + slots * groups
                    tab[low:mid, cols] = jnp.where(live, cosine[rows], 0.0).astype(jnp.bfloat16)
                    tab[mid : low + depth, cols] = jnp.where(live, sine[rows], 0.0).astype(
                        jnp.bfloat16
                    )
                cosine, sine = (
                    cosine * turn_cos - sine * turn_sin,
                    sine * turn_cos + cosine * turn_sin,
                )
            state[0], state[1] = cosine, sine
            table = tab[...]
            grid = jnp.dot(left[...], table, preferred_element_type=jnp.float32)
            made = []
            for u in range(block):
                part = [
                    grid[u * width + f * 2 * layers : u * width + (f + 1) * 2 * layers]
                    for f in range(fields)
                ]
                absolute = part[2] + cor[u]
                made += [
                    absolute * part[0],
                    absolute * part[1],
                    0.5 * (part[0] * part[0] + part[1] * part[1]),
                    part[0] * part[3],
                ]
            if padded > size:
                made.append(jnp.zeros((padded - size, chunk), jnp.float32))
            products = jnp.concatenate(made, 0).astype(jnp.bfloat16)
            acc[...] += lax.dot_general(table, products, NT, preferred_element_type=jnp.float32)
            return carry

        longest = lengths[-1]
        lax.fori_loop(0, (longest + chunk - 1) // chunk, walk, 0)
        for u in range(block):
            at = u * width
            column = at // LANES * LANES
            offset = at % LANES
            north = quad_ref[dist[u]]
            south = quad_ref[total_lat - 1 - dist[u]]
            scale = jnp.where(south_lane, south, north) / floats[u]
            joined = jnp.zeros((groups, LANES), jnp.float32)
            for part in range(2):
                for slot in range(slots):
                    home = (slot * 2 + part) * width
                    row = u * depth + (part * slots + slot) * groups
                    value = acc[row : row + groups, column : column + LANES]
                    shift = (home - offset) % LANES
                    value = pltpu.roll(value, shift, 1) if shift else value
                    keep = (lane >= home) & (lane < home + width)
                    keep = keep & (2.0 * waves[slot] < floats[u])
                    joined = joined + jnp.where(keep, -value if part else value, 0.0)
            joined = joined * scale
            put_refs[0][pl.ds(local[u], groups, stride=count), :] = joined
            put_refs[1][pl.ds(count - 1 - local[u], groups, stride=count), :] = joined
        return carry

    lax.fori_loop(0, count // block, group, 0)


def grid_scratch(dims):
    slots, groups, block = dims["slots"], dims["groups"], dims["block"]
    rows = block * slots * groups
    padded = -(-block * dims["fields"] * 2 * dims["layers"] // LANES) * LANES
    return [
        pltpu.VMEM((2, rows, LANES), jnp.float32),
        pltpu.VMEM((2, rows, LANES), jnp.float32),
        pltpu.VMEM((2 * rows, TILES * LANES), jnp.bfloat16),
        pltpu.VMEM((padded, 2 * rows), jnp.bfloat16),
        pltpu.VMEM((2 * rows, padded), jnp.float32),
        pltpu.VMEM((2 * rows, padded), jnp.float32),
    ]


def final_stage(dims, get, leg_ref, perm_ref):
    slots, columns, half = dims["slots"], dims["columns"], dims["half"]
    turned = lax.dot_general(
        perm_ref[...], get, NT, preferred_element_type=jnp.float32
    ).astype(jnp.bfloat16)
    results = []
    for slot in range(slots):
        total = 0.0
        for hemi in range(2):
            at = (slot * 2 + hemi) * columns
            total += jnp.dot(
                turned[at : at + columns],
                leg_ref[slot, hemi * half : (hemi + 1) * half, :],
                preferred_element_type=jnp.float32,
            )
        results.append(total)
    return results


def joined_rows(dims, back_ref):
    quarter, groups = dims["quarter"], dims["groups"]
    low = [back_ref[place][:quarter] for place in range(groups)]
    high = [back_ref[place][quarter:] for place in reversed(range(groups))]
    return low + high


def first_kernel(dims, spec_ref, leg_ref, live_ref, perm_ref, out_ref, rows_ref):
    fourier_stage(dims, spec_ref, leg_ref, live_ref, perm_ref, rows_ref)
    split_rows(dims, rows_ref, out_ref)


def middle_kernel(dims, recv_ref, waves_ref, quad_ref, cor_ref, out_ref, get, north, south, *scratch):
    groups, count = dims["groups"], 2 * dims["quarter"]
    for source in range(groups):
        get[source * count : (source + 1) * count, :] = recv_ref[source].astype(jnp.float32)
    waves = [waves_ref[slot] for slot in range(dims["slots"])]
    device = lax.axis_index("wave")
    grid_stage(dims, device, waves, quad_ref, cor_ref, get, (north, south), scratch)
    hemi = lax.broadcasted_iota(jnp.int32, (count, LANES), 1) // dims["layers"] % 2
    for source in range(groups):
        rows = slice(source * count, (source + 1) * count)
        out_ref[source] = jnp.where(hemi == 1, south[rows], north[rows]).astype(jnp.bfloat16)


def last_kernel(dims, back_ref, leg_ref, live_ref, perm_ref, geo_ref, out_ref):
    rows = [piece.astype(jnp.float32) for piece in joined_rows(dims, back_ref)]
    get = jnp.concatenate(rows, 0).astype(jnp.bfloat16)
    for slot, value in enumerate(final_stage(dims, get, leg_ref, perm_ref)):
        live = live_ref[slot].astype(jnp.float32)
        out_ref[slot] = ((value + geo_ref[slot]) * live).astype(jnp.bfloat16)


def body(spec, legendre, layer_depth_share, quad_weight, wave_of_slot):
    slots, columns, degrees = spec.shape
    total_lat = legendre.shape[1]
    groups = lax.axis_size("wave")
    layers = layer_depth_share.shape[0]
    quarter = total_lat // groups // 4
    depth = 2 * slots * groups
    block = max(b for b in range(1, quarter + 1) if quarter % b == 0 and b * depth <= max(256, depth))
    dims = dict(
        slots=slots, columns=columns, half=total_lat // 2, groups=groups, layers=layers,
        fields=columns // (2 * layers), quarter=quarter, block=block,
    )
    fields = dims["fields"]
    maps = lane_maps(slots, fields, layers)
    perm = np.zeros((LANES, LANES), np.float32)
    perm[maps, np.arange(LANES)] = 1.0
    perm = jnp.asarray(perm, jnp.bfloat16)
    lat = np.arange(total_lat)
    coriolis = jnp.asarray(2.0 * np.cos(np.pi * (lat + 0.5) / total_lat), jnp.float32)
    all_waves = lax.all_gather(wave_of_slot, "wave")
    waves = jnp.broadcast_to(
        all_waves.T.astype(jnp.float32)[:, :, None], (slots, groups, LANES)
    )
    degree = jnp.arange(degrees, dtype=jnp.int32)
    alive = degree[None, None, :] < (degrees - wave_of_slot)[:, None, None]
    live = alive.astype(jnp.bfloat16)
    thermal = jnp.where(alive, spec, 0).reshape(slots, 2, fields, layers, degrees)[:, :, 3]
    scaled = thermal.astype(jnp.float32) * layer_depth_share[None, None, :, None]
    below = jnp.flip(jnp.cumsum(jnp.flip(scaled, 2), 2), 2)
    parts = lax.all_gather(below[:, :, 0], "lev")
    place = jnp.arange(parts.shape[0]) > lax.axis_index("lev")
    deeper = jnp.sum(jnp.where(place[:, None, None, None], parts, 0.0), 0)
    geopot = below + deeper[:, :, None]
    geo = jnp.zeros((slots, 2, fields, layers, degrees), jnp.float32)
    geo = geo.at[:, :, 2].set(geopot).reshape(slots, columns, degrees)
    vmem = pl.BlockSpec(memory_space=pltpu.VMEM)
    smem = pl.BlockSpec(memory_space=pltpu.SMEM)
    count = 2 * quarter
    send = pl.pallas_call(
        functools.partial(first_kernel, dims),
        out_shape=jax.ShapeDtypeStruct((groups, count, LANES), jnp.bfloat16),
        in_specs=[vmem] * 4,
        out_specs=vmem,
        scratch_shapes=[pltpu.VMEM((dims["half"], LANES), jnp.float32)],
    )(spec, legendre, live, perm)
    recv = lax.all_to_all(send, "wave", 0, 0)
    flat = pltpu.VMEM((groups * count, LANES), jnp.float32)
    out = pl.pallas_call(
        functools.partial(middle_kernel, dims),
        out_shape=jax.ShapeDtypeStruct((groups, count, LANES), jnp.bfloat16),
        in_specs=[vmem, vmem, smem, smem],
        out_specs=vmem,
        scratch_shapes=[flat, flat, flat] + grid_scratch(dims),
    )(recv, waves, quad_weight, coriolis)
    back = lax.all_to_all(out, "wave", 0, 0)
    return pl.pallas_call(
        functools.partial(last_kernel, dims),
        out_shape=jax.ShapeDtypeStruct(spec.shape, jnp.bfloat16),
        in_specs=[vmem] * 5,
        out_specs=vmem,
    )(back, legendre, live, perm, geo)


def solution(mesh):
    in_specs = (P("wave", "lev", None), P("wave", None, None), P("lev"), P(), P("wave"))
    out_specs = P("wave", "lev", None)
    return jax.shard_map(body, mesh=mesh, in_specs=in_specs, out_specs=out_specs, check_vma=False)
```

```python
import functools
import math

import jax
import jax.numpy as jnp
import numpy as np
from jax import lax
from jax.experimental import pallas as pl
from jax.experimental.pallas import tpu as pltpu
from jax.sharding import PartitionSpec as P

TILES = 4
LANES = 128
NT = (((1,), (1,)), ((), ()))


def taylor(first, count):
    return [(-1.0) ** k / math.factorial(2 * k + first) for k in range(count)]


def horner(square, terms):
    total = jnp.full_like(square, terms[-1])
    for term in reversed(terms[:-1]):
        total = total * square + term
    return total


def turn_trig(steps, length, inverse):
    whole = jnp.floor(steps * inverse + 0.5)
    angle = (steps - whole * length) * inverse * (2.0 * math.pi)
    square = angle * angle
    return horner(square, taylor(0, 10)), angle * horner(square, taylor(1, 10))


def lane_maps(slots, fields, layers):
    order = np.arange(slots * 2 * 2 * fields * layers)
    natural = order.reshape(slots, 2, 2, fields, layers)
    return natural.transpose(0, 2, 3, 1, 4).reshape(-1)


def fourier_stage(dims, spec_ref, leg_ref, loads, live, perm_ref, rows_ref):
    slots, columns, half = dims["slots"], dims["columns"], dims["half"]
    total = jnp.zeros((half, LANES), jnp.float32)
    for slot in range(slots):
        masked = spec_ref[slot] * live[slot].astype(jnp.bfloat16)
        for hemi in range(2):
            at = (slot * 2 + hemi) * columns
            pieces = []
            if at:
                pieces.append(jnp.zeros((at, masked.shape[1]), masked.dtype))
            pieces.append(masked)
            if at + columns < LANES:
                pieces.append(jnp.zeros((LANES - at - columns, masked.shape[1]), masked.dtype))
            loads[slot * 2 + hemi].wait()
            total += lax.dot_general(
                leg_ref[slot, hemi * half : (hemi + 1) * half, :],
                jnp.concatenate(pieces, 0),
                NT,
                preferred_element_type=jnp.float32,
            )
    rows_ref[...] = jnp.dot(
        total.astype(jnp.bfloat16), perm_ref[...], preferred_element_type=jnp.float32
    )


def split_rows(dims, rows_ref, send_ref):
    quarter, half = dims["quarter"], dims["half"]
    for place in range(dims["groups"]):
        low = rows_ref[place * quarter : (place + 1) * quarter, :]
        top = half - place * quarter
        high = rows_ref[top - quarter : top, :]
        send_ref[place] = jnp.concatenate([low, high], 0).astype(jnp.bfloat16)


def grid_stage(dims, device, waves, quad_ref, cor_ref, get_ref, put_refs, scratch):
    slots, groups, half = dims["slots"], dims["groups"], dims["half"]
    fields, layers, quarter = dims["fields"], dims["layers"], dims["quarter"]
    block, total_lat = dims["block"], 2 * half
    count = 2 * quarter
    width = fields * 2 * layers
    depth = 2 * slots * groups
    state, step, tab, left, mixed, acc = scratch
    chunk = TILES * LANES
    lane = lax.broadcasted_iota(jnp.int32, (groups, LANES), 1)
    south_lane = lane // layers % 2 == 1
    tile_lane = lax.broadcasted_iota(jnp.int32, (slots * groups, LANES), 1)
    tile_lane_f = tile_lane.astype(jnp.float32)
    hemi_row = lax.broadcasted_iota(jnp.int32, (2 * layers, 1), 0) < layers
    size = block * width
    padded = left.shape[0]
    eye = (
        lax.broadcasted_iota(jnp.int32, (padded, padded), 0)
        == lax.broadcasted_iota(jnp.int32, (padded, padded), 1)
    ).astype(jnp.bfloat16)
    mixed[...] = jnp.zeros_like(mixed)
    all_waves = jnp.concatenate(waves, 0)

    def group(number, carry):
        first = number * block
        local = [first + u for u in range(block)]
        dist = [
            jnp.where(r < quarter, device * quarter + r, half - device * quarter - count + r)
            for r in local
        ]
        lengths = [20 + 4 * q for q in dist]
        floats = [length.astype(jnp.float32) for length in lengths]
        for u in range(block):
            inverse = 1.0 / jnp.full((slots * groups, LANES), floats[u], jnp.float32)
            rows = pl.ds(u * slots * groups, slots * groups)
            base = turn_trig(all_waves * tile_lane_f, floats[u], inverse)
            hop = turn_trig(all_waves * float(LANES), floats[u], inverse)
            for part in range(2):
                state[part, rows, :] = base[part]
                step[part, rows, :] = hop[part]
            north = get_ref[pl.ds(local[u], groups, stride=count), :]
            south = get_ref[pl.ds(count - 1 - local[u], groups, stride=count), :]
            both = jnp.where(south_lane, south, north)
            at = u * width
            column = at // LANES * LANES
            offset = at % LANES
            for part in range(2):
                for slot in range(slots):
                    home = (slot * 2 + part) * width
                    wave = waves[slot]
                    weight = jnp.where(wave == 0.0, 1.0, 2.0)
                    weight = jnp.where(2.0 * wave < floats[u], weight, 0.0)
                    if part:
                        weight = -weight
                    shift = (offset - home) % LANES
                    moved = pltpu.roll(both, shift, 1) if shift else both
                    keep = (lane >= offset) & (lane < offset + width)
                    row = u * depth + (part * slots + slot) * groups
                    mixed[row : row + groups, column : column + LANES] = jnp.where(
                        keep, moved * weight, 0.0
                    )
        left[...] = lax.dot_general(
            eye, mixed[...].astype(jnp.bfloat16), NT, preferred_element_type=jnp.float32
        ).astype(jnp.bfloat16)
        acc[...] = jnp.zeros_like(acc)
        cor = [
            jnp.where(hemi_row, cor_ref[dist[u]], cor_ref[total_lat - 1 - dist[u]])
            for u in range(block)
        ]

        def walk(index, carry):
            cosine, sine = state[0], state[1]
            turn_cos, turn_sin = step[0], step[1]
            for t in range(TILES):
                start = index * chunk + t * LANES
                point = tile_lane + start
                for u in range(block):
                    rows = slice(u * slots * groups, (u + 1) * slots * groups)
                    live = point < lengths[u]
                    cols = slice(t * LANES, (t + 1) * LANES)
                    low = u * depth
                    mid = low + slots * groups
                    tab[low:mid, cols] = jnp.where(live, cosine[rows], 0.0).astype(jnp.bfloat16)
                    tab[mid : low + depth, cols] = jnp.where(live, sine[rows], 0.0).astype(
                        jnp.bfloat16
                    )
                cosine, sine = (
                    cosine * turn_cos - sine * turn_sin,
                    sine * turn_cos + cosine * turn_sin,
                )
            state[0], state[1] = cosine, sine
            table = tab[...]
            grid = jnp.dot(left[...], table, preferred_element_type=jnp.float32)
            made = []
            for u in range(block):
                part = [
                    grid[u * width + f * 2 * layers : u * width + (f + 1) * 2 * layers]
                    for f in range(fields)
                ]
                absolute = part[2] + cor[u]
                made += [
                    absolute * part[0],
                    absolute * part[1],
                    0.5 * (part[0] * part[0] + part[1] * part[1]),
                    part[0] * part[3],
                ]
            if padded > size:
                made.append(jnp.zeros((padded - size, chunk), jnp.float32))
            products = jnp.concatenate(made, 0).astype(jnp.bfloat16)
            acc[...] += lax.dot_general(table, products, NT, preferred_element_type=jnp.float32)
            return carry

        longest = lengths[-1]
        lax.fori_loop(0, (longest + chunk - 1) // chunk, walk, 0)
        for u in range(block):
            at = u * width
            column = at // LANES * LANES
            offset = at % LANES
            north = quad_ref[dist[u]]
            south = quad_ref[total_lat - 1 - dist[u]]
            scale = jnp.where(south_lane, south, north) / floats[u]
            joined = jnp.zeros((groups, LANES), jnp.float32)
            for part in range(2):
                for slot in range(slots):
                    home = (slot * 2 + part) * width
                    row = u * depth + (part * slots + slot) * groups
                    value = acc[row : row + groups, column : column + LANES]
                    shift = (home - offset) % LANES
                    value = pltpu.roll(value, shift, 1) if shift else value
                    keep = (lane >= home) & (lane < home + width)
                    keep = keep & (2.0 * waves[slot] < floats[u])
                    joined = joined + jnp.where(keep, -value if part else value, 0.0)
            joined = joined * scale
            put_refs[0][pl.ds(local[u], groups, stride=count), :] = joined
            put_refs[1][pl.ds(count - 1 - local[u], groups, stride=count), :] = joined
        return carry

    lax.fori_loop(0, count // block, group, 0)


def grid_scratch(dims):
    slots, groups, block = dims["slots"], dims["groups"], dims["block"]
    rows = block * slots * groups
    padded = -(-block * dims["fields"] * 2 * dims["layers"] // LANES) * LANES
    return [
        pltpu.VMEM((2, rows, LANES), jnp.float32),
        pltpu.VMEM((2, rows, LANES), jnp.float32),
        pltpu.VMEM((2 * rows, TILES * LANES), jnp.bfloat16),
        pltpu.VMEM((padded, 2 * rows), jnp.bfloat16),
        pltpu.VMEM((2 * rows, padded), jnp.float32),
        pltpu.VMEM((2 * rows, padded), jnp.float32),
    ]


def final_stage(dims, get, leg_ref, perm_ref):
    slots, columns, half = dims["slots"], dims["columns"], dims["half"]
    turned = lax.dot_general(
        perm_ref[...], get, NT, preferred_element_type=jnp.float32
    ).astype(jnp.bfloat16)
    results = []
    for slot in range(slots):
        total = 0.0
        for hemi in range(2):
            at = (slot * 2 + hemi) * columns
            total += jnp.dot(
                turned[at : at + columns],
                leg_ref[slot, hemi * half : (hemi + 1) * half, :],
                preferred_element_type=jnp.float32,
            )
        results.append(total)
    return results


def joined_rows(dims, back_ref):
    quarter, groups = dims["quarter"], dims["groups"]
    low = [back_ref[place][:quarter] for place in range(groups)]
    high = [back_ref[place][quarter:] for place in reversed(range(groups))]
    return low + high


def to_peer(axis, shift):
    place = lax.axis_index(axis)
    count = lax.axis_size(axis)
    return {axis: lax.rem(place + shift, count)}


def exchange(axis, source_of, target_of, sems):
    place = lax.axis_index(axis)
    count = lax.axis_size(axis)
    copies = []
    for shift in range(1, count):
        peer = lax.rem(place + shift, count)
        copies.append(
            pltpu.make_async_remote_copy(
                src_ref=source_of(peer),
                dst_ref=target_of(place),
                send_sem=sems[0].at[shift],
                recv_sem=sems[1].at[shift],
                device_id=to_peer(axis, shift),
                device_id_type=pl.DeviceIdType.MESH,
            )
        )
    return copies


def whole_kernel(
    dims, spec_ref, leg_hbm, perm_ref, share_ref, quad_ref, cor_ref, wave_ref, out_ref,
    leg, rows, send, recv, back_send, back, wave_send, wave_recv, sum_send, sum_recv, geo,
    get, north, south, load_sem, sem_a, sem_b, sem_c, sem_d, sem_e, sem_f, sem_g, sem_h, *scratch,
):
    slots, groups, half = dims["slots"], dims["groups"], dims["half"]
    fields, layers, count = dims["fields"], dims["layers"], 2 * dims["quarter"]
    degrees = spec_ref.shape[2]
    me = lax.axis_index("wave")
    floor = lax.axis_index("lev")
    floors = lax.axis_size("lev")
    loads = []
    for slot in range(slots):
        for hemi in range(2):
            piece = pl.ds(hemi * half, half)
            copy = pltpu.make_async_copy(
                leg_hbm.at[slot, piece], leg.at[slot, piece], load_sem.at[slot * 2 + hemi]
            )
            copy.start()
            loads.append(copy)
    barrier = pltpu.get_barrier_semaphore()
    for axis, size in (("wave", groups), ("lev", floors)):
        for shift in range(1, size):
            pl.semaphore_signal(
                barrier, inc=1, device_id=to_peer(axis, shift), device_id_type=pl.DeviceIdType.MESH
            )
    degree = lax.broadcasted_iota(jnp.int32, (1, degrees), 1)
    live = [
        jnp.where(degree < degrees - wave_ref[slot], 1.0, 0.0).astype(jnp.float32)
        for slot in range(slots)
    ]
    row = lax.broadcasted_iota(jnp.int32, (8, LANES), 0)
    own = jnp.zeros((8, LANES), jnp.float32)
    for slot in range(slots):
        own = jnp.where(row == slot, wave_ref[slot].astype(jnp.float32), own)
    wave_send[...] = own
    geo[...] = jnp.zeros_like(geo)
    for slot in range(slots):
        full = spec_ref[slot].astype(jnp.float32) * live[slot]
        for part in range(2):
            first = part * fields * layers
            total = jnp.zeros((1, degrees), jnp.float32)
            for layer in reversed(range(layers)):
                at = first + 3 * layers + layer
                total = total + full[at : at + 1] * share_ref[layer]
                at = first + 2 * layers + layer
                geo[slot, at : at + 1, :] = total
            at = slot * 2 + part
            sum_send[at : at + 1, :] = total
    pl.semaphore_wait(barrier, groups - 1 + floors - 1)

    def wave_place(device):
        return wave_recv.at[pl.ds(pl.multiple_of(device * 8, 8), 8)]

    tell = exchange("wave", lambda _: wave_send, wave_place, (sem_a, sem_b))
    lift = exchange("lev", lambda _: sum_send, lambda p: sum_recv.at[p], (sem_c, sem_d))
    for copy in tell + lift:
        copy.start()
    wave_recv[pl.ds(pl.multiple_of(me * 8, 8), 8), :] = own
    fourier_stage(dims, spec_ref, leg, loads, live, perm_ref, rows)
    split_rows(dims, rows, send)
    there = exchange("wave", lambda p: send.at[p], lambda p: recv.at[p], (sem_e, sem_f))
    for copy in there:
        copy.start()
    recv[me] = send[me]
    for copy in tell:
        copy.wait()
    waves = [wave_recv[pl.ds(slot, groups, stride=8), :] for slot in range(slots)]
    for copy in there:
        copy.wait()
    for source in range(groups):
        get[source * count : (source + 1) * count, :] = recv[source].astype(jnp.float32)
    grid_stage(dims, me, waves, quad_ref, cor_ref, get, (north, south), scratch)
    hemi = lax.broadcasted_iota(jnp.int32, (count, LANES), 1) // layers % 2
    for source in range(groups):
        piece = slice(source * count, (source + 1) * count)
        back_send[source] = jnp.where(hemi == 1, south[piece], north[piece]).astype(jnp.bfloat16)
    home = exchange("wave", lambda p: back_send.at[p], lambda p: back.at[p], (sem_g, sem_h))
    for copy in home:
        copy.start()
    back[me] = back_send[me]
    for copy in lift:
        copy.wait()
    for slot in range(slots):
        for part in range(2):
            at = slot * 2 + part
            deeper = jnp.zeros((1, degrees), jnp.float32)
            for other in range(floors):
                value = sum_recv[other, at : at + 1, :]
                deeper = deeper + jnp.where(other > floor, value, 0.0)
            first = (part * fields + 2) * layers
            geo[slot, first : first + layers, :] += deeper
    for copy in home:
        copy.wait()
    pieces = [piece.astype(jnp.float32) for piece in joined_rows(dims, back)]
    joined = jnp.concatenate(pieces, 0).astype(jnp.bfloat16)
    for slot, value in enumerate(final_stage(dims, joined, leg, perm_ref)):
        out_ref[slot] = ((value + geo[slot]) * live[slot]).astype(jnp.bfloat16)


def body(spec, legendre, layer_depth_share, quad_weight, wave_of_slot):
    slots, columns, degrees = spec.shape
    total_lat = legendre.shape[1]
    groups = lax.axis_size("wave")
    layers = layer_depth_share.shape[0]
    quarter = total_lat // groups // 4
    depth = 2 * slots * groups
    block = max(b for b in range(1, quarter + 1) if quarter % b == 0 and b * depth <= max(256, depth))
    dims = dict(
        slots=slots, columns=columns, half=total_lat // 2, groups=groups, layers=layers,
        fields=columns // (2 * layers), quarter=quarter, block=block,
    )
    fields = dims["fields"]
    maps = lane_maps(slots, fields, layers)
    perm = np.zeros((LANES, LANES), np.float32)
    perm[maps, np.arange(LANES)] = 1.0
    perm = jnp.asarray(perm, jnp.bfloat16)
    lat = np.arange(total_lat)
    coriolis = jnp.asarray(2.0 * np.cos(np.pi * (lat + 0.5) / total_lat), jnp.float32)
    floors = lax.axis_size("lev")
    half, count = total_lat // 2, 2 * quarter
    vmem = pl.BlockSpec(memory_space=pltpu.VMEM)
    smem = pl.BlockSpec(memory_space=pltpu.SMEM)
    rows = pltpu.VMEM((groups, count, LANES), jnp.bfloat16)
    flat = pltpu.VMEM((groups * count, LANES), jnp.float32)
    sums = 2 * slots
    return pl.pallas_call(
        functools.partial(whole_kernel, dims),
        out_shape=jax.ShapeDtypeStruct(spec.shape, jnp.bfloat16),
        in_specs=[vmem, pl.BlockSpec(memory_space=pl.ANY), vmem] + [smem] * 4,
        out_specs=vmem,
        scratch_shapes=[
            pltpu.VMEM(legendre.shape, jnp.bfloat16),
            pltpu.VMEM((half, LANES), jnp.float32),
            rows, rows, rows, rows,
            pltpu.VMEM((8, LANES), jnp.float32),
            pltpu.VMEM((groups * 8, LANES), jnp.float32),
            pltpu.VMEM((sums, degrees), jnp.float32),
            pltpu.VMEM((floors, sums, degrees), jnp.float32),
            pltpu.VMEM(spec.shape, jnp.float32),
            flat, flat, flat,
            pltpu.SemaphoreType.DMA((2 * slots,)),
            pltpu.SemaphoreType.DMA((groups,)),
            pltpu.SemaphoreType.DMA((groups,)),
            pltpu.SemaphoreType.DMA((floors,)),
            pltpu.SemaphoreType.DMA((floors,)),
            pltpu.SemaphoreType.DMA((groups,)),
            pltpu.SemaphoreType.DMA((groups,)),
            pltpu.SemaphoreType.DMA((groups,)),
            pltpu.SemaphoreType.DMA((groups,)),
        ]
        + grid_scratch(dims),
        compiler_params=pltpu.CompilerParams(collective_id=0, has_side_effects=True),
    )(spec, legendre, perm, layer_depth_share, quad_weight, coriolis, wave_of_slot)


def solution(mesh):
    in_specs = (P("wave", "lev", None), P("wave", None, None), P("lev"), P(), P("wave"))
    out_specs = P("wave", "lev", None)
    return jax.shard_map(body, mesh=mesh, in_specs=in_specs, out_specs=out_specs, check_vma=False)
```

```python
import functools
import math

import jax
import jax.numpy as jnp
import numpy as np
from jax import lax
from jax.experimental import pallas as pl
from jax.experimental.pallas import tpu as pltpu
from jax.sharding import PartitionSpec as P

TILES = 10
SUB = 2
LANES = 128
NT = (((1,), (1,)), ((), ()))


def taylor(first, count):
    return [(-1.0) ** k / math.factorial(2 * k + first) for k in range(count)]


def horner(square, terms):
    total = jnp.full_like(square, terms[-1])
    for term in reversed(terms[:-1]):
        total = total * square + term
    return total


def turn_trig(steps, length, inverse):
    whole = jnp.floor(steps * inverse + 0.5)
    angle = (steps - whole * length) * inverse * (2.0 * math.pi)
    square = angle * angle
    return horner(square, taylor(0, 10)), angle * horner(square, taylor(1, 10))


def lane_maps(slots, fields, layers):
    order = np.arange(slots * 2 * 2 * fields * layers)
    natural = order.reshape(slots, 2, 2, fields, layers)
    return natural.transpose(0, 2, 3, 1, 4).reshape(-1)


def fourier_stage(dims, spec_ref, leg_ref, loads, live, perm_ref, rows_ref):
    slots, columns, half = dims["slots"], dims["columns"], dims["half"]
    total = jnp.zeros((half, LANES), jnp.float32)
    for slot in range(slots):
        masked = spec_ref[slot] * live[slot].astype(jnp.bfloat16)
        for hemi in range(2):
            at = (slot * 2 + hemi) * columns
            pieces = []
            if at:
                pieces.append(jnp.zeros((at, masked.shape[1]), masked.dtype))
            pieces.append(masked)
            if at + columns < LANES:
                pieces.append(jnp.zeros((LANES - at - columns, masked.shape[1]), masked.dtype))
            loads[slot * 2 + hemi].wait()
            total += lax.dot_general(
                leg_ref[slot, hemi * half : (hemi + 1) * half, :],
                jnp.concatenate(pieces, 0),
                NT,
                preferred_element_type=jnp.float32,
            )
    rows_ref[...] = jnp.dot(
        total.astype(jnp.bfloat16), perm_ref[...], preferred_element_type=jnp.float32
    )


def split_rows(dims, rows_ref, send_ref):
    quarter, half = dims["quarter"], dims["half"]
    for place in range(dims["groups"]):
        low = rows_ref[place * quarter : (place + 1) * quarter, :]
        top = half - place * quarter
        high = rows_ref[top - quarter : top, :]
        send_ref[place] = jnp.concatenate([low, high], 0).astype(jnp.bfloat16)


def whereabouts(dims, device, number):
    quarter, block = dims["quarter"], dims["block"]
    local = [number * block + u for u in range(block)]
    dist = [
        jnp.where(
            r < quarter, device * quarter + r, dims["half"] - (device + 2) * quarter + r
        )
        for r in local
    ]
    lengths = [20 + 4 * q for q in dist]
    return local, dist, lengths, [length.astype(jnp.float32) for length in lengths]


def trig_stage(dims, device, waves, base, step):
    rows = dims["slots"] * dims["groups"]
    all_waves = jnp.concatenate(waves, 0)
    lane = lax.broadcasted_iota(jnp.int32, (rows, LANES), 1).astype(jnp.float32)

    def group(number, carry):
        floats = whereabouts(dims, device, number)[3]
        for u, length in enumerate(floats):
            inverse = 1.0 / jnp.full((rows, LANES), length, jnp.float32)
            begin = turn_trig(all_waves * lane, length, inverse)
            hop = turn_trig(all_waves * float(LANES), length, inverse)
            for part in range(2):
                base[number, part, u * rows : (u + 1) * rows, :] = begin[part]
                step[number, part, u * rows : (u + 1) * rows, :] = hop[part]
        return carry

    lax.fori_loop(0, 2 * dims["quarter"] // dims["block"], group, 0)


def grid_stage(dims, device, waves, quad_ref, cor_ref, get_ref, put_refs, scratch):
    slots, groups, half = dims["slots"], dims["groups"], dims["half"]
    fields, layers, quarter = dims["fields"], dims["layers"], dims["quarter"]
    block, total_lat = dims["block"], 2 * half
    count = 2 * quarter
    width = fields * 2 * layers
    depth = 2 * slots * groups
    base, step, state, tab, left, mixed, acc = scratch
    chunk = TILES * LANES
    lane = lax.broadcasted_iota(jnp.int32, (groups, LANES), 1)
    south_lane = lane // layers % 2 == 1
    tile_lane = lax.broadcasted_iota(jnp.int32, (slots * groups, LANES), 1)
    hemi_row = lax.broadcasted_iota(jnp.int32, (2 * layers, 1), 0) < layers
    size = block * width
    padded = left.shape[0]
    eye = (
        lax.broadcasted_iota(jnp.int32, (padded, padded), 0)
        == lax.broadcasted_iota(jnp.int32, (padded, padded), 1)
    ).astype(jnp.bfloat16)
    mixed[...] = jnp.zeros_like(mixed)

    def group(number, carry):
        local, dist, lengths, floats = whereabouts(dims, device, number)
        for u in range(block):
            north = get_ref[pl.ds(local[u], groups, stride=count), :]
            south = get_ref[pl.ds(count - 1 - local[u], groups, stride=count), :]
            both = jnp.where(south_lane, south, north)
            at = u * width
            column = at // LANES * LANES
            offset = at % LANES
            for part in range(2):
                for slot in range(slots):
                    home = (slot * 2 + part) * width
                    wave = waves[slot]
                    weight = jnp.where(wave == 0.0, 1.0, 2.0)
                    weight = jnp.where(2.0 * wave < floats[u], weight, 0.0)
                    if part:
                        weight = -weight
                    shift = (offset - home) % LANES
                    moved = pltpu.roll(both, shift, 1) if shift else both
                    keep = (lane >= offset) & (lane < offset + width)
                    row = u * depth + (part * slots + slot) * groups
                    mixed[row : row + groups, column : column + LANES] = jnp.where(
                        keep, moved * weight, 0.0
                    )
        left[...] = lax.dot_general(
            eye, mixed[...].astype(jnp.bfloat16), NT, preferred_element_type=jnp.float32
        ).astype(jnp.bfloat16)
        acc[...] = jnp.zeros_like(acc)
        state[...] = base[number]
        cor = [
            jnp.where(hemi_row, cor_ref[dist[u]], cor_ref[total_lat - 1 - dist[u]])
            for u in range(block)
        ]

        def walk(index, carry):
            turn_cos, turn_sin = step[number, 0], step[number, 1]

            def fill(t, cosine, sine):
                point = tile_lane + (index * chunk + t * LANES)
                cols = slice(t * LANES, (t + 1) * LANES)
                for u in range(block):
                    rows = slice(u * slots * groups, (u + 1) * slots * groups)
                    live = point < lengths[u]
                    low = u * depth
                    mid = low + slots * groups
                    tab[low:mid, cols] = jnp.where(live, cosine[rows], 0.0).astype(jnp.bfloat16)
                    tab[mid : low + depth, cols] = jnp.where(live, sine[rows], 0.0).astype(
                        jnp.bfloat16
                    )
                return (
                    cosine * turn_cos - sine * turn_sin,
                    sine * turn_cos + cosine * turn_sin,
                )

            def use(first, last):
                table = tab[:, first * LANES : last * LANES]
                grid = jnp.dot(left[...], table, preferred_element_type=jnp.float32)
                made = []
                for u in range(block):
                    part = [
                        grid[u * width + f * 2 * layers : u * width + (f + 1) * 2 * layers]
                        for f in range(fields)
                    ]
                    absolute = part[2] + cor[u]
                    made += [
                        absolute * part[0],
                        absolute * part[1],
                        0.5 * (part[0] * part[0] + part[1] * part[1]),
                        part[0] * part[3],
                    ]
                if padded > size:
                    made.append(jnp.zeros((padded - size, table.shape[1]), jnp.float32))
                products = jnp.concatenate(made, 0).astype(jnp.bfloat16)
                return lax.dot_general(table, products, NT, preferred_element_type=jnp.float32)

            cosine, sine = state[0], state[1]
            total = acc[...]
            edges = list(range(0, TILES, SUB)) + [TILES]
            spans = list(zip(edges[:-1], edges[1:]))
            for t in range(*spans[0]):
                cosine, sine = fill(t, cosine, sine)
            for span, following in zip(spans, spans[1:] + [None]):
                if following:
                    for t in range(*following):
                        cosine, sine = fill(t, cosine, sine)
                total = total + use(*span)
            state[0], state[1] = cosine, sine
            acc[...] = total
            return carry

        longest = lengths[-1]
        lax.fori_loop(0, (longest + chunk - 1) // chunk, walk, 0)
        for u in range(block):
            at = u * width
            column = at // LANES * LANES
            offset = at % LANES
            north = quad_ref[dist[u]]
            south = quad_ref[total_lat - 1 - dist[u]]
            scale = jnp.where(south_lane, south, north) / floats[u]
            joined = jnp.zeros((groups, LANES), jnp.float32)
            for part in range(2):
                for slot in range(slots):
                    home = (slot * 2 + part) * width
                    row = u * depth + (part * slots + slot) * groups
                    value = acc[row : row + groups, column : column + LANES]
                    shift = (home - offset) % LANES
                    value = pltpu.roll(value, shift, 1) if shift else value
                    keep = (lane >= home) & (lane < home + width)
                    keep = keep & (2.0 * waves[slot] < floats[u])
                    joined = joined + jnp.where(keep, -value if part else value, 0.0)
            joined = joined * scale
            put_refs[0][pl.ds(local[u], groups, stride=count), :] = joined
            put_refs[1][pl.ds(count - 1 - local[u], groups, stride=count), :] = joined
        return carry

    lax.fori_loop(0, count // block, group, 0)


def grid_scratch(dims):
    slots, groups, block = dims["slots"], dims["groups"], dims["block"]
    rows = block * slots * groups
    padded = -(-block * dims["fields"] * 2 * dims["layers"] // LANES) * LANES
    number = 2 * dims["quarter"] // block
    return [
        pltpu.VMEM((number, 2, rows, LANES), jnp.float32),
        pltpu.VMEM((number, 2, rows, LANES), jnp.float32),
        pltpu.VMEM((2, rows, LANES), jnp.float32),
        pltpu.VMEM((2 * rows, TILES * LANES), jnp.bfloat16),
        pltpu.VMEM((padded, 2 * rows), jnp.bfloat16),
        pltpu.VMEM((2 * rows, padded), jnp.float32),
        pltpu.VMEM((2 * rows, padded), jnp.float32),
    ]


def final_stage(dims, get, leg_ref, perm_ref):
    slots, columns, half = dims["slots"], dims["columns"], dims["half"]
    turned = lax.dot_general(
        perm_ref[...], get, NT, preferred_element_type=jnp.float32
    ).astype(jnp.bfloat16)
    results = []
    for slot in range(slots):
        total = 0.0
        for hemi in range(2):
            at = (slot * 2 + hemi) * columns
            total += jnp.dot(
                turned[at : at + columns],
                leg_ref[slot, hemi * half : (hemi + 1) * half, :],
                preferred_element_type=jnp.float32,
            )
        results.append(total)
    return results


def joined_rows(dims, back_ref):
    quarter, groups = dims["quarter"], dims["groups"]
    low = [back_ref[place][:quarter] for place in range(groups)]
    high = [back_ref[place][quarter:] for place in reversed(range(groups))]
    return low + high


def to_peer(axis, shift):
    place = lax.axis_index(axis)
    count = lax.axis_size(axis)
    return {axis: lax.rem(place + shift, count)}


def exchange(axis, source_of, target_of, sems):
    place = lax.axis_index(axis)
    count = lax.axis_size(axis)
    copies = []
    for shift in range(1, count):
        peer = lax.rem(place + shift, count)
        copies.append(
            pltpu.make_async_remote_copy(
                src_ref=source_of(peer),
                dst_ref=target_of(place),
                send_sem=sems[0].at[shift],
                recv_sem=sems[1].at[shift],
                device_id=to_peer(axis, shift),
                device_id_type=pl.DeviceIdType.MESH,
            )
        )
    return copies


def whole_kernel(
    dims, spec_ref, leg_hbm, perm_ref, share_ref, quad_ref, cor_ref, wave_ref, out_ref,
    leg, rows, send, recv, back_send, back, wave_send, wave_recv, sum_send, sum_recv, geo,
    get, north, south, load_sem, sem_a, sem_b, sem_c, sem_d, sem_e, sem_f, sem_g, sem_h, *scratch,
):
    slots, groups, half = dims["slots"], dims["groups"], dims["half"]
    fields, layers, count = dims["fields"], dims["layers"], 2 * dims["quarter"]
    degrees = spec_ref.shape[2]
    me = lax.axis_index("wave")
    floor = lax.axis_index("lev")
    floors = lax.axis_size("lev")
    loads = []
    for slot in range(slots):
        for hemi in range(2):
            piece = pl.ds(hemi * half, half)
            copy = pltpu.make_async_copy(
                leg_hbm.at[slot, piece], leg.at[slot, piece], load_sem.at[slot * 2 + hemi]
            )
            copy.start()
            loads.append(copy)
    barrier = pltpu.get_barrier_semaphore()
    for axis, size in (("wave", groups), ("lev", floors)):
        for shift in range(1, size):
            pl.semaphore_signal(
                barrier, inc=1, device_id=to_peer(axis, shift), device_id_type=pl.DeviceIdType.MESH
            )
    degree = lax.broadcasted_iota(jnp.int32, (1, degrees), 1)
    live = [
        jnp.where(degree < degrees - wave_ref[slot], 1.0, 0.0).astype(jnp.float32)
        for slot in range(slots)
    ]
    row = lax.broadcasted_iota(jnp.int32, (8, LANES), 0)
    own = jnp.zeros((8, LANES), jnp.float32)
    for slot in range(slots):
        own = jnp.where(row == slot, wave_ref[slot].astype(jnp.float32), own)
    wave_send[...] = own
    geo[...] = jnp.zeros_like(geo)
    for slot in range(slots):
        full = spec_ref[slot].astype(jnp.float32) * live[slot]
        for part in range(2):
            first = part * fields * layers
            total = jnp.zeros((1, degrees), jnp.float32)
            for layer in reversed(range(layers)):
                at = first + 3 * layers + layer
                total = total + full[at : at + 1] * share_ref[layer]
                at = first + 2 * layers + layer
                geo[slot, at : at + 1, :] = total
            at = slot * 2 + part
            sum_send[at : at + 1, :] = total
    fourier_stage(dims, spec_ref, leg, loads, live, perm_ref, rows)
    split_rows(dims, rows, send)
    pl.semaphore_wait(barrier, groups - 1 + floors - 1)

    def wave_place(device):
        return wave_recv.at[pl.ds(pl.multiple_of(device * 8, 8), 8)]

    tell = exchange("wave", lambda _: wave_send, wave_place, (sem_a, sem_b))
    lift = exchange("lev", lambda _: sum_send, lambda p: sum_recv.at[p], (sem_c, sem_d))
    for copy in tell:
        copy.start()
    wave_recv[pl.ds(pl.multiple_of(me * 8, 8), 8), :] = own
    there = exchange("wave", lambda p: send.at[p], lambda p: recv.at[p], (sem_e, sem_f))
    for copy in there + lift:
        copy.start()
    recv[me] = send[me]
    for copy in tell:
        copy.wait()
    waves = [wave_recv[pl.ds(slot, groups, stride=8), :] for slot in range(slots)]
    trig_stage(dims, me, waves, scratch[0], scratch[1])
    for copy in there:
        copy.wait()
    for source in range(groups):
        get[source * count : (source + 1) * count, :] = recv[source].astype(jnp.float32)
    grid_stage(dims, me, waves, quad_ref, cor_ref, get, (north, south), scratch)
    hemi = lax.broadcasted_iota(jnp.int32, (count, LANES), 1) // layers % 2
    for source in range(groups):
        piece = slice(source * count, (source + 1) * count)
        back_send[source] = jnp.where(hemi == 1, south[piece], north[piece]).astype(jnp.bfloat16)
    home = exchange("wave", lambda p: back_send.at[p], lambda p: back.at[p], (sem_g, sem_h))
    for copy in home:
        copy.start()
    back[me] = back_send[me]
    for copy in lift:
        copy.wait()
    for slot in range(slots):
        for part in range(2):
            at = slot * 2 + part
            deeper = jnp.zeros((1, degrees), jnp.float32)
            for other in range(floors):
                value = sum_recv[other, at : at + 1, :]
                deeper = deeper + jnp.where(other > floor, value, 0.0)
            first = (part * fields + 2) * layers
            geo[slot, first : first + layers, :] += deeper
    for copy in home:
        copy.wait()
    pieces = [piece.astype(jnp.float32) for piece in joined_rows(dims, back)]
    joined = jnp.concatenate(pieces, 0).astype(jnp.bfloat16)
    for slot, value in enumerate(final_stage(dims, joined, leg, perm_ref)):
        out_ref[slot] = ((value + geo[slot]) * live[slot]).astype(jnp.bfloat16)


def body(spec, legendre, layer_depth_share, quad_weight, wave_of_slot):
    slots, columns, degrees = spec.shape
    total_lat = legendre.shape[1]
    groups = lax.axis_size("wave")
    layers = layer_depth_share.shape[0]
    quarter = total_lat // groups // 4
    depth = 2 * slots * groups
    block = max(b for b in range(1, quarter + 1) if quarter % b == 0 and b * depth <= max(256, depth))
    dims = dict(
        slots=slots, columns=columns, half=total_lat // 2, groups=groups, layers=layers,
        fields=columns // (2 * layers), quarter=quarter, block=block,
    )
    fields = dims["fields"]
    maps = lane_maps(slots, fields, layers)
    perm = np.zeros((LANES, LANES), np.float32)
    perm[maps, np.arange(LANES)] = 1.0
    perm = jnp.asarray(perm, jnp.bfloat16)
    lat = np.arange(total_lat)
    coriolis = jnp.asarray(2.0 * np.cos(np.pi * (lat + 0.5) / total_lat), jnp.float32)
    floors = lax.axis_size("lev")
    half, count = total_lat // 2, 2 * quarter
    vmem = pl.BlockSpec(memory_space=pltpu.VMEM)
    smem = pl.BlockSpec(memory_space=pltpu.SMEM)
    rows = pltpu.VMEM((groups, count, LANES), jnp.bfloat16)
    flat = pltpu.VMEM((groups * count, LANES), jnp.float32)
    sums = 2 * slots
    return pl.pallas_call(
        functools.partial(whole_kernel, dims),
        out_shape=jax.ShapeDtypeStruct(spec.shape, jnp.bfloat16),
        in_specs=[vmem, pl.BlockSpec(memory_space=pl.ANY), vmem] + [smem] * 4,
        out_specs=vmem,
        scratch_shapes=[
            pltpu.VMEM(legendre.shape, jnp.bfloat16),
            pltpu.VMEM((half, LANES), jnp.float32),
            rows, rows, rows, rows,
            pltpu.VMEM((8, LANES), jnp.float32),
            pltpu.VMEM((groups * 8, LANES), jnp.float32),
            pltpu.VMEM((sums, degrees), jnp.float32),
            pltpu.VMEM((floors, sums, degrees), jnp.float32),
            pltpu.VMEM(spec.shape, jnp.float32),
            flat, flat, flat,
            pltpu.SemaphoreType.DMA((2 * slots,)),
            pltpu.SemaphoreType.DMA((groups,)),
            pltpu.SemaphoreType.DMA((groups,)),
            pltpu.SemaphoreType.DMA((floors,)),
            pltpu.SemaphoreType.DMA((floors,)),
            pltpu.SemaphoreType.DMA((groups,)),
            pltpu.SemaphoreType.DMA((groups,)),
            pltpu.SemaphoreType.DMA((groups,)),
            pltpu.SemaphoreType.DMA((groups,)),
        ]
        + grid_scratch(dims),
        compiler_params=pltpu.CompilerParams(collective_id=0, has_side_effects=True),
    )(spec, legendre, perm, layer_depth_share, quad_weight, coriolis, wave_of_slot)


def solution(mesh):
    in_specs = (P("wave", "lev", None), P("wave", None, None), P("lev"), P(), P("wave"))
    out_specs = P("wave", "lev", None)
    return jax.shard_map(body, mesh=mesh, in_specs=in_specs, out_specs=out_specs, check_vma=False)
```
